32 devices in a mesh: space: 4 (over z), chan: 8 (over y, x, core).
Axes of the slice: x: 2, y: 2, z: 4, core: 2. Of those that a mesh axis runs over, the one named last changes fastest.
Arguments:
- inputs: bfloat16 [1024, 8, 128], P('chan', 'space'), may hold values from -6 to 6
- conv_out: bfloat16 [1024, 8, 128], P('chan', 'space'), may hold values from -90 to 90
- upstream: bfloat16 [1024, 8, 128], P('chan', 'space'), may hold values from -100 to 100
- weights: bfloat16 [27, 1024, 1024], P(None, 'chan'), may hold values from -0.0390625 to 0.0390625
- norm_gain: float32 [1024], P('chan'), may hold values from 0.5 to 2
- run_sigma: float32 [1024], P('chan'), may hold values from 0.3 to 30
Outputs:
- input_grad: bfloat16 [1024, 8, 128], P('chan', 'space')
- weight_grad: float32 [27, 1024, 1024], P(None, 'chan', 'space')
The draws below stay inside these ranges and needn't reach their ends.
All inputs are finite; a program needn't handle non-finite values.
Results may differ from the reference program's by a relative error of at most 0.005.
Values may be sent and summed in bfloat16 or wider, within the bound.
A program may use at most 128 MiB of HBM per device.

```python
import math
import jax
import jax.numpy as jnp
from jax import lax

C = 1024
H = 8
W = 16
ND = 8
PLANE = 128


def depth_ramp():
    depth_pos = jnp.arange(ND, dtype=jnp.float32)
    return (3.0 ** (depth_pos / max(ND - 1, 1)))[None, :, None]


def conv_shape(key):
    keys = jax.random.split(jax.random.fold_in(key, 17), 4)
    base = jax.random.truncated_normal(keys[0], -4.0, 4.0, (C, ND, PLANE), jnp.float32)
    return (base, keys)


def signed_factor(key):
    sub_keys = jax.random.split(key, 2)
    magnitude = jnp.exp(jax.random.uniform(sub_keys[0], (C, 1, 1), jnp.float32, math.log(0.3), math.log(1.0)))
    signs = jnp.where(jax.random.bernoulli(sub_keys[1], 0.5, (C, 1, 1)), 1.0, -1.0)
    return magnitude * signs


def draw_conv_out(key, part):
    shape, keys = conv_shape(key)
    chan_scale = jnp.exp(jax.random.uniform(keys[2], (C, 1, 1), jnp.float32, math.log(0.5), math.log(4.0)))
    offset = jax.random.uniform(keys[3], (C, 1, 1), jnp.float32, -1.0, 1.0) * chan_scale
    return (shape * chan_scale * depth_ramp() + offset).astype(jnp.bfloat16)


def draw_upstream(key, part):
    shape, unused = conv_shape(key)
    keys = jax.random.split(jax.random.fold_in(key, 29), 5)
    base = jax.random.truncated_normal(keys[0], -4.0, 4.0, (C, ND, PLANE), jnp.float32)
    along = signed_factor(keys[3])
    offset = signed_factor(keys[4])
    return ((base + along * shape) * depth_ramp() + offset).astype(jnp.bfloat16)


def shard_levels(rng, extent, pieces, least, high):
    def one(axis_at, blocks):
        steps = jax.random.uniform(jax.random.fold_in(jax.random.fold_in(rng, 6), axis_at), (blocks,), jnp.float32, least / len(pieces), high / len(pieces))
        return jnp.repeat(jnp.exp(steps), extent[axis_at] // blocks).reshape((-1,) + (1,) * (len(extent) - axis_at - 1))

    factor_of = one(*pieces[0])
    for cut in pieces[1:]:
        factor_of = factor_of * one(*cut)
    return factor_of


def bell_draw(key, dims, spread, bound, pieces=(), held_as=jnp.bfloat16):
    array = spread * jax.random.normal(key, dims, jnp.float32)
    if pieces:
        array = array * shard_levels(key, dims, pieces, -0.22, 0.18)
    return jnp.clip(array, -bound, bound).astype(held_as)


def setup_inputs(seed: int = 0) -> dict:
    key_of = jax.random.split(jax.random.key(seed), 7)
    return {
        "inputs": bell_draw(key_of[0], (C, ND, PLANE), 1.0, 6.0, ((0, 8), (1, 4))),
        "conv_out": draw_conv_out(jax.random.fold_in(key_of[6], 71), 0),
        "upstream": draw_upstream(jax.random.fold_in(key_of[6], 71), 0),
        "weights": bell_draw(key_of[3], (27, C, C), (27 * C) ** -0.5, 0.0390625, ((1, 8),)),
        "norm_gain": jnp.clip(jnp.exp(math.log(2.0) - 1.3862944 * jax.random.uniform(key_of[4], (C,), jnp.float32) ** shard_levels(key_of[4], (C,), ((0, 8),), -0.2, 0.2)), 0.5, 2.0),
        "run_sigma": jnp.clip(jnp.exp(math.log(30.0) - 4.6051701 * jax.random.uniform(key_of[5], (C,), jnp.float32) ** shard_levels(key_of[5], (C,), ((0, 8),), -0.2, 0.2)), 0.3, 30.0),
    }


epsilon = 1e-05
clip_limit = 3.0
taps_list = [(tap // 9, tap // 3 % 3, tap % 3) for tap in range(27)]

def reference(inputs, conv_out, upstream, weights, norm_gain, run_sigma):
    outputs_f = conv_out.astype(jnp.float32)
    mean_val = lax.optimization_barrier(jnp.mean(outputs_f, axis=(1, 2)))
    centred = outputs_f - mean_val[:, None, None]
    var_val = lax.optimization_barrier(jnp.mean(centred * centred, axis=(1, 2)))
    std_dev = jnp.sqrt(var_val + epsilon)
    ratios = jnp.clip(std_dev / run_sigma, 1.0 / clip_limit, clip_limit)
    scaled = upstream.astype(jnp.float32) * norm_gain[:, None, None]
    normed = centred / std_dev[:, None, None]
    mean_up = lax.optimization_barrier(jnp.mean(scaled, axis=(1, 2)))
    mean_cross = lax.optimization_barrier(jnp.mean(scaled * normed, axis=(1, 2)))
    out_grad = ((ratios / std_dev)[:, None, None] * (scaled - mean_up[:, None, None] - normed * mean_cross[:, None, None])).astype(jnp.bfloat16)
    channels, planes, plane_len = inputs.shape
    grad_wide = out_grad.astype(jnp.float32)
    grad_pad = jnp.pad(grad_wide.reshape(channels, planes, H, W), ((0, 0), (1, 1), (1, 1), (1, 1)))
    input_pad = jnp.pad(inputs.astype(jnp.float32).reshape(channels, planes, H, W), ((0, 0), (1, 1), (1, 1), (1, 1)))
    grad_flat = grad_wide.reshape(channels, planes * plane_len)
    weights_wide = weights.astype(jnp.float32)
    accumulated = jnp.zeros((channels, planes * plane_len), jnp.float32)
    weight_terms = []
    for depth_off, row_off, col_off in taps_list:
        tap_index = 9 * depth_off + 3 * row_off + col_off
        shifted = grad_pad[:, 2 - depth_off:2 - depth_off + planes, 2 - row_off:2 - row_off + H, 2 - col_off:2 - col_off + W].reshape(channels, planes * plane_len)
        accumulated = accumulated + jnp.dot(weights_wide[tap_index], shifted, precision=lax.Precision.HIGHEST)
        shifted_in = input_pad[:, depth_off:depth_off + planes, row_off:row_off + H, col_off:col_off + W].reshape(channels, planes * plane_len)
        weight_terms.append(jnp.dot(shifted_in, grad_flat.T, precision=lax.Precision.HIGHEST))
    return (accumulated.reshape(channels, planes, plane_len).astype(jnp.bfloat16), jnp.stack(weight_terms))
```

```python
import functools

import jax
import jax.numpy as jnp
from jax import lax
from jax.experimental import pallas as pl
from jax.experimental.pallas import tpu as pltpu
from jax.sharding import PartitionSpec as P

H = 8
W = 16
LANES = 128

epsilon = 1e-05
clip_limit = 3.0


def exchange(ns, per, inp, conv, up, gain, sigma, ga, gb, g2, xall, sbuf, stats, *sems):
    (st_s, st_r, x_s, x_r, a_s, a_r, ap_s, ap_r, f_s, f_r, z_s, z_r, zp_s, zp_r,
     r_s, r_r, b_s, b_r, bp_s, bp_r, bf_s, bf_r) = sems
    s = lax.axis_index("space")
    c = lax.axis_index("chan")
    k = c // per
    h = c % per
    cb, pw = inp.shape
    n_local = pw

    def send(src, dst, ss, rs, sp, ch):
        copy = pltpu.make_async_remote_copy(
            src_ref=src, dst_ref=dst, send_sem=ss, recv_sem=rs,
            device_id={"space": sp, "chan": ch}, device_id_type=pl.DeviceIdType.MESH,
        )
        return copy

    barrier = pltpu.get_barrier_semaphore()
    space_peers = [lax.rem(s + e, ns) for e in range(1, ns)]
    group_peers = [lax.rem(k + d, ns) * per + h for d in range(1, ns)]
    partners = [k * per + lax.rem(h + j, per) for j in range(1, per)]
    for sp in space_peers:
        pl.semaphore_signal(barrier, inc=1, device_id={"space": sp, "chan": c}, device_id_type=pl.DeviceIdType.MESH)
    for ch in group_peers + partners:
        pl.semaphore_signal(barrier, inc=1, device_id={"space": s, "chan": ch}, device_id_type=pl.DeviceIdType.MESH)

    x = conv[...].astype(jnp.float32)
    u = up[...].astype(jnp.float32)
    m_col = jnp.sum(x, axis=1, keepdims=True) * (1.0 / n_local)
    xc = x - m_col
    m2_col = jnp.sum(xc * xc, axis=1, keepdims=True)
    su_col = jnp.sum(u, axis=1, keepdims=True)
    cux_col = jnp.sum(u * xc, axis=1, keepdims=True)
    lane = lax.broadcasted_iota(jnp.int32, (cb, LANES), 1)
    packed = jnp.where(lane == 0, m_col, jnp.where(lane == 1, m2_col, jnp.where(lane == 2, su_col, jnp.where(lane == 3, cux_col, 0.0))))
    rows = gain.shape[1]
    if rows > cb:
        packed = jnp.concatenate([packed, jnp.zeros((rows - cb, LANES), jnp.float32)], axis=0)
    flipped = packed.T[:8]
    sbuf[...] = flipped

    own_cols = pl.ds(pl.multiple_of(s * pw, LANES), pw)
    pl.semaphore_wait(barrier, 2 * (ns - 1) + per - 1)
    st_copies = [send(sbuf, stats.at[s], st_s.at[e], st_r.at[e], space_peers[e - 1], c) for e in range(1, ns)]
    for copy in st_copies:
        copy.start()
    x_copies = [send(inp, xall.at[:, own_cols], x_s.at[e], x_r.at[e], space_peers[e - 1], c) for e in range(1, ns)]
    stats[pl.ds(s, 1)] = flipped[None]
    xall[:, own_cols] = inp[...]
    for copy in st_copies:
        copy.wait_recv()

    alls = [stats[i] for i in range(ns)]
    mean = functools.reduce(lambda p, q: p + q, [t[0:1] for t in alls]) * (1.0 / ns)
    dev = [t[0:1] - mean for t in alls]
    m2 = functools.reduce(lambda p, q: p + q, [t[1:2] for t in alls])
    m2 = m2 + float(n_local) * functools.reduce(lambda p, q: p + q, [d * d for d in dev])
    cells = float(n_local * ns)
    var_eps = m2 * (1.0 / cells) + epsilon
    std = jnp.sqrt(var_eps)
    mean_up = functools.reduce(lambda p, q: p + q, [t[2:3] for t in alls]) * (1.0 / cells)
    cross = functools.reduce(lambda p, q: p + q, [t[3:4] + t[2:3] * d for t, d in zip(alls, dev)]) * (1.0 / cells)
    ratio = jnp.clip(std / sigma[...], 1.0 / clip_limit, clip_limit)
    front = ratio / std * gain[...]
    slope = cross / var_eps
    sub = lax.broadcasted_iota(jnp.int32, (LANES, rows), 0)
    coef = jnp.where(sub == 0, mean, jnp.where(sub == 1, mean_up, jnp.where(sub == 2, front, jnp.where(sub == 3, slope, 0.0))))
    coef = coef.T[:cb]
    grad = coef[:, 2:3] * (u - coef[:, 1:2] - (x - coef[:, 0:1]) * coef[:, 3:4])
    block = pl.ds(pl.multiple_of(c * cb, cb), cb)
    ga[block, :] = grad.astype(jnp.bfloat16)

    lo = pl.ds(0, LANES)
    hi = pl.ds(LANES, LANES)
    up_copy = send(ga.at[block, pl.ds(pw - LANES, LANES)], gb.at[block, lo], r_s.at[0], r_r.at[0], lax.rem(s + 1, ns), c)
    down_copy = send(ga.at[block, pl.ds(0, LANES)], gb.at[block, hi], r_s.at[1], r_r.at[1], lax.rem(s + ns - 1, ns), c)

    @pl.when(s < ns - 1)
    def _():
        up_copy.start()

    @pl.when(s > 0)
    def _():
        down_copy.start()

    a_copies = [send(ga.at[block], ga.at[block], a_s.at[d], a_r.at[d], s, group_peers[d - 1]) for d in range(1, ns)]
    ap_copies = [send(ga.at[block], ga.at[block], ap_s.at[j], ap_r.at[j], s, partners[j - 1]) for j in range(1, per)]
    for copy in a_copies + ap_copies:
        copy.start()
    for copy in x_copies:
        copy.start()

    @pl.when(s == 0)
    def _():
        gb[block, lo] = jnp.zeros((cb, LANES), jnp.bfloat16)

    @pl.when(s == ns - 1)
    def _():
        gb[block, hi] = jnp.zeros((cb, LANES), jnp.bfloat16)

    @pl.when(s > 0)
    def _():
        up_copy.wait_recv()

    @pl.when(s < ns - 1)
    def _():
        down_copy.wait_recv()

    for copy in a_copies:
        copy.wait_recv()

    def rows_of(kk, hh):
        return pl.ds(pl.multiple_of((kk * per + hh) * cb, cb), cb)

    my_rows = pl.ds(pl.multiple_of(h * cb, cb), cb)
    z_copies = [
        send(ga.at[rows_of(space_peers[e - 1], h)], g2.at[my_rows, own_cols], z_s.at[e], z_r.at[e], space_peers[e - 1], c)
        for e in range(1, ns)
    ]
    for copy in z_copies:
        copy.start()
    b_copies = [send(gb.at[block], gb.at[block], b_s.at[d], b_r.at[d], s, group_peers[d - 1]) for d in range(1, ns)]
    bp_copies = [send(gb.at[block], gb.at[block], bp_s.at[j], bp_r.at[j], s, partners[j - 1]) for j in range(1, per)]
    for copy in b_copies + bp_copies:
        copy.start()

    def forwards(ref, ss, rs):
        out = []
        for d in range(1, ns):
            piece = rows_of(lax.rem(k + ns - d, ns), h)
            for j in range(1, per):
                out.append(send(ref.at[piece], ref.at[piece], ss.at[d, j], rs.at[d, j], s, partners[j - 1]))
        return out

    f_copies = forwards(ga, f_s, f_r)
    for copy in f_copies:
        copy.start()
    for copy in b_copies:
        copy.wait_recv()
    bf_copies = forwards(gb, bf_s, bf_r)
    for copy in bf_copies:
        copy.start()
    zp_copies = []
    for e in range(1, ns):
        z_copies[e - 1].wait_recv()
        cols = pl.ds(pl.multiple_of(lax.rem(s + ns - e, ns) * pw, LANES), pw)
        for j in range(1, per):
            copy = send(g2.at[my_rows, cols], g2.at[my_rows, cols], zp_s.at[e, j], zp_r.at[e, j], s, partners[j - 1])
            copy.start()
            zp_copies.append(copy)
    for copy in ap_copies + f_copies:
        copy.wait_recv()
    g2[:, own_cols] = ga[pl.ds(pl.multiple_of(s * (per * cb), per * cb), per * cb), :]
    for copy in x_copies + bp_copies + bf_copies + zp_copies:
        copy.wait_recv()
    for copy in st_copies + x_copies + a_copies + ap_copies + f_copies + z_copies + zp_copies + b_copies + bp_copies + bf_copies:
        copy.wait_send()

    @pl.when(s < ns - 1)
    def _():
        up_copy.wait_send()

    @pl.when(s > 0)
    def _():
        down_copy.wait_send()


def moved(plane, row_off, col_off, sign):
    row_off, col_off = sign * row_off, sign * col_off
    delta = row_off * W + col_off
    if delta == 0:
        return plane
    width = plane.shape[1]
    out = pltpu.roll(plane, (-delta) % width, 1)
    cell = lax.broadcasted_iota(jnp.int32, plane.shape, 1)
    row = cell // W + row_off
    col = cell % W + col_off
    return jnp.where((row >= 0) & (row < H) & (col >= 0) & (col < W), out, 0.0)


def products(ns, w, ga, gb, g2, xall, ig, wg, gp, xs, acc):
    a = pl.program_id(0)
    cb, total = xall.shape
    pw = ga.shape[1]
    planes = pw // LANES
    depth = total // LANES

    @pl.when(a == 0)
    def _():
        gp[:, 0:LANES] = gb[:, 0:LANES]
        gp[:, LANES : LANES + pw] = ga[...]
        gp[:, LANES + pw :] = gb[:, LANES:]
        zero = jnp.zeros((9 * cb, LANES), jnp.bfloat16)
        xs[:, 0:LANES] = zero
        xs[:, LANES + total :] = zero
        for d in range(depth):
            plane = xall[:, d * LANES : (d + 1) * LANES].astype(jnp.float32)
            for b in range(3):
                for e in range(3):
                    at = (3 * b + e) * cb
                    xs[at : at + cb, (d + 1) * LANES : (d + 2) * LANES] = moved(plane, b - 1, e - 1, 1).astype(jnp.bfloat16)

    shifted = xs[:, pl.ds(pl.multiple_of(a * LANES, LANES), total)]
    wgrad = lax.dot_general(shifted, g2[...], (((1,), (1,)), ((), ())), preferred_element_type=jnp.float32)
    wg[...] = wgrad.reshape(wg.shape)
    rhs = gp[:, pl.ds(pl.multiple_of((2 - a) * LANES, LANES), pw)]
    part = jnp.dot(w[...].reshape(9 * cb, w.shape[2]), rhs, preferred_element_type=jnp.float32)

    @pl.when(a == 0)
    def _():
        acc[...] = part

    @pl.when(a > 0)
    def _():
        acc[...] += part

    @pl.when(a == 2)
    def _():
        for p in range(planes):
            out = jnp.zeros((cb, LANES), jnp.float32)
            for b in range(3):
                for e in range(3):
                    at = (3 * b + e) * cb
                    out = out + moved(acc[at : at + cb, p * LANES : (p + 1) * LANES], b - 1, e - 1, -1)
            ig[:, p * LANES : (p + 1) * LANES] = out.astype(jnp.bfloat16)


def solution(mesh):
    ns = mesh.shape["space"]
    nc = mesh.shape["chan"]
    per = nc // ns

    def on_device(inputs, conv_out, upstream, weights, norm_gain, run_sigma):
        cb, planes, plane_len = inputs.shape
        pw = planes * plane_len
        channels = cb * nc
        rows = max(cb, LANES)

        def flat(t):
            return t.reshape(cb, pw)

        def row(t):
            return jnp.pad(t, (0, rows - cb), constant_values=1.0).reshape(1, rows)

        vmem = pl.BlockSpec(memory_space=pltpu.VMEM)
        dma = pltpu.SemaphoreType.DMA
        sem_shapes = []
        for shape in ((ns,), (ns,), (ns,), (per,), (ns, per), (ns,), (ns, per), (2,), (ns,), (per,), (ns, per)):
            sem_shapes += [dma(shape), dma(shape)]
        bf = jnp.bfloat16
        ga, gb, g2, xall = pl.pallas_call(
            functools.partial(exchange, ns, per),
            out_shape=(
                jax.ShapeDtypeStruct((channels, pw), bf),
                jax.ShapeDtypeStruct((channels, 2 * LANES), bf),
                jax.ShapeDtypeStruct((per * cb, ns * pw), bf),
                jax.ShapeDtypeStruct((cb, ns * pw), bf),
            ),
            in_specs=[vmem] * 5,
            out_specs=(vmem,) * 4,
            scratch_shapes=[pltpu.VMEM((8, rows), jnp.float32), pltpu.VMEM((ns, 8, rows), jnp.float32)] + sem_shapes,
            compiler_params=pltpu.CompilerParams(collective_id=0, has_side_effects=True),
        )(flat(inputs), flat(conv_out), flat(upstream), row(norm_gain), row(run_sigma))

        ig, wg = pl.pallas_call(
            functools.partial(products, ns),
            grid=(3,),
            out_shape=(
                jax.ShapeDtypeStruct((cb, pw), bf),
                jax.ShapeDtypeStruct((27, cb, per * cb), jnp.float32),
            ),
            in_specs=[
                pl.BlockSpec((9, cb, channels), lambda a: (a, 0, 0)),
                vmem, vmem, vmem, vmem,
            ],
            out_specs=(
                pl.BlockSpec((cb, pw), lambda a: (0, 0)),
                pl.BlockSpec((9, cb, per * cb), lambda a: (a, 0, 0)),
            ),
            scratch_shapes=[
                pltpu.VMEM((channels, pw + 2 * LANES), bf),
                pltpu.VMEM((9 * cb, ns * pw + 2 * LANES), bf),
                pltpu.VMEM((9 * cb, pw), jnp.float32),
            ],
        )(weights, ga, gb, g2, xall)
        return ig.reshape(cb, planes, plane_len), wg

    return jax.shard_map(
        on_device,
        mesh=mesh,
        in_specs=(
            P("chan", "space", None),
            P("chan", "space", None),
            P("chan", "space", None),
            P(None, "chan", None),
            P("chan"),
            P("chan"),
        ),
        out_specs=(P("chan", "space", None), P(None, "chan", "space")),
        check_vma=False,
    )
```

```python
import functools

import jax
import jax.numpy as jnp
from jax import lax
from jax.experimental import pallas as pl
from jax.experimental.pallas import tpu as pltpu
from jax.sharding import PartitionSpec as P

H = 8
W = 16
LANES = 128

epsilon = 1e-05
clip_limit = 3.0


def planes_flat(ref):
    return jnp.concatenate([ref[:, p, :].astype(jnp.float32) for p in range(ref.shape[1])], axis=1)


def exchange(ns, per, inp, conv, up, gain, sigma, w, ig, g2, xall, ga, gb, sbuf, stats, xbuf, wbuf, acc, w_sem, *sems):
    (st_s, st_r, x_s, x_r, a_s, a_r, ap_s, ap_r, f_s, f_r, z_s, z_r, zp_s, zp_r,
     r_s, r_r, b_s, b_r, bp_s, bp_r, bf_s, bf_r) = sems
    s = lax.axis_index("space")
    c = lax.axis_index("chan")
    k = c // per
    h = c % per
    cb, planes, _ = inp.shape
    pw = planes * LANES
    n_local = pw
    w_copies = [pltpu.make_async_copy(w.at[pl.ds(9 * a, 9)], wbuf.at[pl.ds(9 * a, 9)], w_sem.at[a]) for a in (1, 2, 0)]
    for copy in w_copies:
        copy.start()

    def send(src, dst, ss, rs, sp, ch):
        copy = pltpu.make_async_remote_copy(
            src_ref=src, dst_ref=dst, send_sem=ss, recv_sem=rs,
            device_id={"space": sp, "chan": ch}, device_id_type=pl.DeviceIdType.MESH,
        )
        return copy

    barrier = pltpu.get_barrier_semaphore()
    space_peers = [lax.rem(s + e, ns) for e in range(1, ns)]
    group_peers = [lax.rem(k + d, ns) * per + h for d in range(1, ns)]
    partners = [k * per + lax.rem(h + j, per) for j in range(1, per)]
    for sp in space_peers:
        pl.semaphore_signal(barrier, inc=1, device_id={"space": sp, "chan": c}, device_id_type=pl.DeviceIdType.MESH)
    for ch in group_peers + partners:
        pl.semaphore_signal(barrier, inc=1, device_id={"space": s, "chan": ch}, device_id_type=pl.DeviceIdType.MESH)

    x = planes_flat(conv)
    u = planes_flat(up)
    xbuf[...] = planes_flat(inp).astype(jnp.bfloat16)
    m_col = jnp.sum(x, axis=1, keepdims=True) * (1.0 / n_local)
    xc = x - m_col
    m2_col = jnp.sum(xc * xc, axis=1, keepdims=True)
    su_col = jnp.sum(u, axis=1, keepdims=True)
    cux_col = jnp.sum(u * xc, axis=1, keepdims=True)
    lane = lax.broadcasted_iota(jnp.int32, (cb, LANES), 1)
    packed = jnp.where(lane == 0, m_col, jnp.where(lane == 1, m2_col, jnp.where(lane == 2, su_col, jnp.where(lane == 3, cux_col, 0.0))))
    rows = gain.shape[1]
    if rows > cb:
        packed = jnp.concatenate([packed, jnp.zeros((rows - cb, LANES), jnp.float32)], axis=0)
    flipped = packed.T[:8]
    sbuf[...] = flipped

    own_cols = pl.ds(pl.multiple_of(s * pw, LANES), pw)
    pl.semaphore_wait(barrier, 2 * (ns - 1) + per - 1)
    st_copies = [send(sbuf, stats.at[s], st_s.at[e], st_r.at[e], space_peers[e - 1], c) for e in range(1, ns)]
    for copy in st_copies:
        copy.start()
    x_copies = [send(xbuf, xall.at[:, own_cols], x_s.at[e], x_r.at[e], space_peers[e - 1], c) for e in range(1, ns)]
    for copy in x_copies:
        copy.start()
    stats[pl.ds(s, 1)] = flipped[None]
    xall[:, own_cols] = xbuf[...]
    for copy in st_copies:
        copy.wait_recv()

    alls = [stats[i] for i in range(ns)]
    mean = functools.reduce(lambda p, q: p + q, [t[0:1] for t in alls]) * (1.0 / ns)
    dev = [t[0:1] - mean for t in alls]
    m2 = functools.reduce(lambda p, q: p + q, [t[1:2] for t in alls])
    m2 = m2 + float(n_local) * functools.reduce(lambda p, q: p + q, [d * d for d in dev])
    cells = float(n_local * ns)
    var_eps = m2 * (1.0 / cells) + epsilon
    std = jnp.sqrt(var_eps)
    mean_up = functools.reduce(lambda p, q: p + q, [t[2:3] for t in alls]) * (1.0 / cells)
    cross = functools.reduce(lambda p, q: p + q, [t[3:4] + t[2:3] * d for t, d in zip(alls, dev)]) * (1.0 / cells)
    ratio = jnp.clip(std / sigma[...], 1.0 / clip_limit, clip_limit)
    front = ratio / std * gain[...]
    slope = cross / var_eps
    sub = lax.broadcasted_iota(jnp.int32, (LANES, rows), 0)
    coef = jnp.where(sub == 0, mean, jnp.where(sub == 1, mean_up, jnp.where(sub == 2, front, jnp.where(sub == 3, slope, 0.0))))
    coef = coef.T[:cb]
    grad = coef[:, 2:3] * (u - coef[:, 1:2] - (x - coef[:, 0:1]) * coef[:, 3:4])
    block = pl.ds(pl.multiple_of(c * cb, cb), cb)
    ga[block, :] = grad.astype(jnp.bfloat16)

    lo = pl.ds(0, LANES)
    hi = pl.ds(LANES, LANES)
    up_copy = send(ga.at[block, pl.ds(pw - LANES, LANES)], gb.at[block, lo], r_s.at[0], r_r.at[0], lax.rem(s + 1, ns), c)
    down_copy = send(ga.at[block, pl.ds(0, LANES)], gb.at[block, hi], r_s.at[1], r_r.at[1], lax.rem(s + ns - 1, ns), c)

    @pl.when(s < ns - 1)
    def _():
        up_copy.start()

    @pl.when(s > 0)
    def _():
        down_copy.start()

    a_copies = [send(ga.at[block], ga.at[block], a_s.at[d], a_r.at[d], s, group_peers[d - 1]) for d in range(1, ns)]
    ap_copies = [send(ga.at[block], ga.at[block], ap_s.at[j], ap_r.at[j], s, partners[j - 1]) for j in range(1, per)]
    for copy in a_copies + ap_copies:
        copy.start()

    @pl.when(s == 0)
    def _():
        gb[block, lo] = jnp.zeros((cb, LANES), jnp.bfloat16)

    @pl.when(s == ns - 1)
    def _():
        gb[block, hi] = jnp.zeros((cb, LANES), jnp.bfloat16)

    @pl.when(s > 0)
    def _():
        up_copy.wait_recv()

    @pl.when(s < ns - 1)
    def _():
        down_copy.wait_recv()

    b_copies = [send(gb.at[block], gb.at[block], b_s.at[d], b_r.at[d], s, group_peers[d - 1]) for d in range(1, ns)]
    bp_copies = [send(gb.at[block], gb.at[block], bp_s.at[j], bp_r.at[j], s, partners[j - 1]) for j in range(1, per)]
    for copy in b_copies + bp_copies:
        copy.start()
    for copy in a_copies:
        copy.wait_recv()

    def rows_of(kk, hh):
        return pl.ds(pl.multiple_of((kk * per + hh) * cb, cb), cb)

    my_rows = pl.ds(pl.multiple_of(h * cb, cb), cb)
    z_copies = [
        send(ga.at[rows_of(space_peers[e - 1], h)], g2.at[my_rows, own_cols], z_s.at[e], z_r.at[e], space_peers[e - 1], c)
        for e in range(1, ns)
    ]
    for copy in z_copies:
        copy.start()
    def forwards(ref, ss, rs):
        out = []
        for d in range(1, ns):
            piece = rows_of(lax.rem(k + ns - d, ns), h)
            for j in range(1, per):
                out.append(send(ref.at[piece], ref.at[piece], ss.at[d, j], rs.at[d, j], s, partners[j - 1]))
        return out

    f_copies = forwards(ga, f_s, f_r)
    for copy in f_copies:
        copy.start()
    def product(a, rhs):
        w_copies[(a + 2) % 3].wait()
        taps = wbuf[9 * a : 9 * a + 9].reshape(9 * cb, wbuf.shape[2])
        return jnp.dot(taps, rhs, preferred_element_type=jnp.float32)

    for copy in ap_copies + f_copies:
        copy.wait_recv()
    acc[...] = product(1, ga[...])
    for copy in b_copies:
        copy.wait_recv()
    bf_copies = forwards(gb, bf_s, bf_r)
    for copy in bf_copies:
        copy.start()
    g2[:, own_cols] = ga[pl.ds(pl.multiple_of(s * (per * cb), per * cb), per * cb), :]
    for copy in bp_copies + bf_copies:
        copy.wait_recv()
    if planes > 1:
        below = jnp.concatenate([gb[:, 0:LANES], ga[:, 0 : pw - LANES]], axis=1)
        above = jnp.concatenate([ga[:, LANES:], gb[:, LANES:]], axis=1)
    else:
        below, above = gb[:, 0:LANES], gb[:, LANES:]
    acc[...] += product(2, below)
    acc[...] += product(0, above)
    zp_copies = []
    for e in range(1, ns):
        z_copies[e - 1].wait_recv()
        cols = pl.ds(pl.multiple_of(lax.rem(s + ns - e, ns) * pw, LANES), pw)
        for j in range(1, per):
            copy = send(g2.at[my_rows, cols], g2.at[my_rows, cols], zp_s.at[e, j], zp_r.at[e, j], s, partners[j - 1])
            copy.start()
            zp_copies.append(copy)
    for p in range(planes):
        out = jnp.zeros((cb, LANES), jnp.float32)
        for b in range(3):
            for e in range(3):
                at = (3 * b + e) * cb
                out = out + moved(acc[at : at + cb, p * LANES : (p + 1) * LANES], b - 1, e - 1, -1)
        ig[:, p * LANES : (p + 1) * LANES] = out.astype(jnp.bfloat16)
    for copy in x_copies + zp_copies:
        copy.wait_recv()
    for copy in st_copies + x_copies + a_copies + ap_copies + f_copies + z_copies + zp_copies + b_copies + bp_copies + bf_copies:
        copy.wait_send()

    @pl.when(s < ns - 1)
    def _():
        up_copy.wait_send()

    @pl.when(s > 0)
    def _():
        down_copy.wait_send()


def moved(plane, row_off, col_off, sign):
    row_off, col_off = sign * row_off, sign * col_off
    delta = row_off * W + col_off
    if delta == 0:
        return plane
    width = plane.shape[1]
    out = pltpu.roll(plane, (-delta) % width, 1)
    cell = lax.broadcasted_iota(jnp.int32, plane.shape, 1)
    row = cell // W + row_off
    col = cell % W + col_off
    return jnp.where((row >= 0) & (row < H) & (col >= 0) & (col < W), out, 0.0)


def products(ig_flat, g2, xall, ig, wg, xs):
    a = pl.program_id(0)
    cb, total = xall.shape
    depth = total // LANES

    @pl.when(a == 0)
    def _():
        zero = jnp.zeros((9 * cb, LANES), jnp.bfloat16)
        xs[:, 0:LANES] = zero
        xs[:, LANES + total :] = zero
        for d in range(depth):
            plane = xall[:, d * LANES : (d + 1) * LANES].astype(jnp.float32)
            for b in range(3):
                for e in range(3):
                    at = (3 * b + e) * cb
                    xs[at : at + cb, (d + 1) * LANES : (d + 2) * LANES] = moved(plane, b - 1, e - 1, 1).astype(jnp.bfloat16)
        planes = ig.shape[1]
        cols = [ig_flat[:, p * LANES : (p + 1) * LANES].astype(jnp.float32) for p in range(planes)]
        ig[...] = jnp.stack(cols, axis=1).astype(jnp.bfloat16)

    shifted = xs[:, pl.ds(pl.multiple_of(a * LANES, LANES), total)]
    wgrad = lax.dot_general(shifted, g2[...], (((1,), (1,)), ((), ())), preferred_element_type=jnp.float32)
    wg[...] = wgrad.reshape(wg.shape)


def solution(mesh):
    ns = mesh.shape["space"]
    nc = mesh.shape["chan"]
    per = nc // ns

    def on_device(inputs, conv_out, upstream, weights, norm_gain, run_sigma):
        cb, planes, plane_len = inputs.shape
        pw = planes * plane_len
        channels = cb * nc
        rows = max(cb, LANES)

        def row(t):
            return jnp.pad(t, (0, rows - cb), constant_values=1.0).reshape(1, rows)

        vmem = pl.BlockSpec(memory_space=pltpu.VMEM)
        dma = pltpu.SemaphoreType.DMA
        sem_shapes = []
        for shape in ((ns,), (ns,), (ns,), (per,), (ns, per), (ns,), (ns, per), (2,), (ns,), (per,), (ns, per)):
            sem_shapes += [dma(shape), dma(shape)]
        bf = jnp.bfloat16
        ig_flat, g2, xall = pl.pallas_call(
            functools.partial(exchange, ns, per),
            out_shape=(
                jax.ShapeDtypeStruct((cb, pw), bf),
                jax.ShapeDtypeStruct((per * cb, ns * pw), bf),
                jax.ShapeDtypeStruct((cb, ns * pw), bf),
            ),
            in_specs=[vmem] * 5 + [pl.BlockSpec(memory_space=pl.ANY)],
            out_specs=(vmem,) * 3,
            scratch_shapes=[
                pltpu.VMEM((channels, pw), bf),
                pltpu.VMEM((channels, 2 * LANES), bf),
                pltpu.VMEM((8, rows), jnp.float32),
                pltpu.VMEM((ns, 8, rows), jnp.float32),
                pltpu.VMEM((cb, pw), bf),
                pltpu.VMEM(weights.shape, bf),
                pltpu.VMEM((9 * cb, pw), jnp.float32),
                dma((3,)),
            ] + sem_shapes,
            compiler_params=pltpu.CompilerParams(collective_id=0, has_side_effects=True),
        )(inputs, conv_out, upstream, row(norm_gain), row(run_sigma), weights)

        ig, wg = pl.pallas_call(
            products,
            grid=(3,),
            out_shape=(
                jax.ShapeDtypeStruct(inputs.shape, bf),
                jax.ShapeDtypeStruct((27, cb, per * cb), jnp.float32),
            ),
            in_specs=[vmem, vmem, vmem],
            out_specs=(
                pl.BlockSpec(inputs.shape, lambda a: (0, 0, 0)),
                pl.BlockSpec((9, cb, per * cb), lambda a: (a, 0, 0)),
            ),
            scratch_shapes=[pltpu.VMEM((9 * cb, ns * pw + 2 * LANES), bf)],
        )(ig_flat, g2, xall)
        return ig, wg

    return jax.shard_map(
        on_device,
        mesh=mesh,
        in_specs=(
            P("chan", "space", None),
            P("chan", "space", None),
            P("chan", "space", None),
            P(None, "chan", None),
            P("chan"),
            P("chan"),
        ),
        out_specs=(P("chan", "space", None), P(None, "chan", "space")),
        check_vma=False,
    )
```
